512 devices in a mesh: mode: 16 (over z_lo, y), cell: 32 (over z_hi, x, core).
Axes of the slice: x: 4, y: 4, z: 16 (z_hi: 4, z_lo: 4; z = z_hi * 4 + z_lo), core: 2. Of those that a mesh axis runs over, the one named last changes fastest.
Arguments:
- populations: float32 [2048, 1, 64, 128], P('mode', None, 'cell'), may hold values from -6 to 6
- contact_mask: int32 [1, 64, 128], P(None, 'cell'), may hold values 0 or 1
- octant: int32 [2048], P('mode'), may hold values from 0 to 7
- courant: float32 [3, 2048], P(None, 'mode'), may hold values from 0.03 to 0.3
- collision: bfloat16 [2048, 2048], P('mode'), as said below
Outputs:
- advanced: float32 [2048, 1, 64, 128], P('mode', None, 'cell')
The draws below stay inside these ranges and needn't reach their ends.
Inputs may be any that keep to these rules, and one draw needn't show every extreme that they name: `collision`: diagonal entries between 0.1 and 0.6, off-diagonal ones small, all independent.
All inputs are finite; a program needn't handle non-finite values. No bound on the sum of `contact_mask` on one device may be relied on, other than what follows from the above.
Results may differ from the reference program's by a relative error of at most 0.0014.
Values may be sent and summed in bfloat16 or wider, within the bound.
A program may use at most 64 MiB of HBM per device.

```python
import math
import jax
import jax.numpy as jnp

MODES = 2048
PLANES = 1
NX = 128
NY = 64


def draw_collision(key, part):
    key_diag = jax.random.fold_in(key, 11)
    key_off = jax.random.fold_in(key, 12)
    diag = jax.random.uniform(key_diag, (MODES,), jnp.float32, 0.1, 0.6)
    off = jax.random.normal(key_off, (MODES, MODES), jnp.float32)
    off = off * (0.2 / math.sqrt(MODES))
    eye = jnp.eye(MODES, dtype=jnp.float32)
    return (off * (1.0 - eye) + eye * diag[:, None]).astype(jnp.bfloat16)


def with_ends(drawn, stream_key, least, high):
    place = [jax.random.randint(jax.random.fold_in(stream_key, axis), (), 0, length) for axis, length in enumerate(drawn.shape)]
    longest = drawn.shape.index(max(drawn.shape))
    beside = place[:longest] + [(place[longest] + 1) % drawn.shape[longest]] + place[longest + 1:]
    return drawn.at[tuple(place)].set(least).at[tuple(beside)].set(high)


def levels(stream_key, shape, shards, least, top_value):
    loudness = 1.0
    for position, blocks in shards:
        steps = jax.random.uniform(jax.random.fold_in(jax.random.fold_in(stream_key, 6), position), (blocks,), jnp.float32, least / len(shards), top_value / len(shards))
        loudness = loudness * jnp.repeat(jnp.exp(steps), shape[position] // blocks).reshape((-1,) + (1,) * (len(shape) - 1 - position))
    return loudness


def normal_values(key, extent, width, reach, split=(), kind=jnp.bfloat16):
    level = levels(key, extent, split, -0.22, 0.18) if split else 1.0
    drawn = jax.random.normal(key, extent, jnp.float32) * width * level
    return jnp.minimum(jnp.maximum(drawn, -reach), reach).astype(kind)


def setup_inputs(seed: int = 0) -> dict:
    key_of = jax.random.split(jax.random.key(seed), 6)
    return {
        "populations": normal_values(key_of[0], (MODES, PLANES, NY, NX), 1.0, 6.0, ((0, 16), (2, 32)), jnp.float32),
        "contact_mask": with_ends((jax.random.randint(key_of[1], (PLANES, NY, NX), 0, 8) < 1).astype(jnp.int32), jax.random.fold_in(key_of[1], 1), 0, 1),
        "octant": with_ends(jax.random.randint(key_of[2], (MODES,), 0, 8), jax.random.fold_in(key_of[2], 1), 0, 7).astype(jnp.int32),
        "courant": jnp.clip(jnp.exp(math.log(0.3) - 2.3025852 * jax.random.uniform(key_of[3], (3, MODES), jnp.float32) ** levels(key_of[3], (3, MODES), ((1, 16),), -0.2, 0.2)), 0.03, 0.3),
        "collision": draw_collision(jax.random.fold_in(key_of[5], 71), 0),
    }


def velocities(octant, courant):
    bits = [octant % 2, (octant // 2) % 2, (octant // 4) % 2]
    return [(1.0 - 2.0 * bits[d].astype(jnp.float32)) * courant[d] for d in range(3)]


def advect(field, speeds):
    vx, vy, vz = [s[:, None, None, None] for s in speeds]
    back_x = jnp.roll(field, 1, axis=3)
    ahead_x = jnp.roll(field, -1, axis=3)
    padded_y = jnp.pad(field, ((0, 0), (0, 0), (1, 1), (0, 0)))
    padded_z = jnp.pad(field, ((0, 0), (1, 1), (0, 0), (0, 0)))
    total = jnp.maximum(vx, 0.0) * (field - back_x) + jnp.minimum(vx, 0.0) * (ahead_x - field)
    total = total + jnp.maximum(vy, 0.0) * (field - padded_y[:, :, :-2]) + jnp.minimum(vy, 0.0) * (padded_y[:, :, 2:] - field)
    total = total + jnp.maximum(vz, 0.0) * (field - padded_z[:, :-2]) + jnp.minimum(vz, 0.0) * (padded_z[:, 2:] - field)
    return total


def collide(field, collision):
    rounded = field.astype(jnp.bfloat16).reshape(field.shape[0], -1)
    return jnp.dot(collision, rounded, preferred_element_type=jnp.float32).reshape(field.shape)


def reference(populations, contact_mask, octant, courant, collision):
    keep = (1 - contact_mask).astype(jnp.float32)[None]
    speeds = velocities(octant, courant)
    first = keep * populations
    second = keep * (first - advect(first, speeds) - collide(first, collision))
    final = second - advect(second, speeds) - collide(second, collision)
    return keep * (0.5 * first + 0.5 * final)
```

```python
import jax
import jax.numpy as jnp
from jax import lax
from jax.experimental import pallas as pl
from jax.experimental.pallas import tpu as pltpu
from jax.sharding import PartitionSpec as P


B = 128
MESH = pl.DeviceIdType.MESH
F32, BF16 = jnp.float32, jnp.bfloat16


def kernel(
    pop_hbm, mask_hbm, octant_hbm, courant_hbm, coll_hbm, out_ref,
    pop, mask, octant, courant, speed, blocks, gathered, halo, sums, outgoing, incoming, field,
    load_sem, block_sem, blocks_send, blocks_recv, gather_send, gather_recv, halo_send, halo_recv, part_send, part_recv,
):
    mode, cell = lax.axis_index("mode"), lax.axis_index("cell")
    y, zl = mode % 4, mode // 4
    core, x, zh = cell % 2, cell // 2 % 4, cell // 8
    g = (1 - core) * y + core * zl
    s = (1 - core) * zl + core * y

    def on_gather_axis(place):
        return (1 - core) * (zl * 4 + place) + core * (place * 4 + y)

    def on_scatter_axis(place):
        return (1 - core) * (place * 4 + y) + core * (zl * 4 + place)

    def shifted_z(shift):
        z = (zh * 4 + zl + shift + 16) % 16
        return z % 4 * 4 + y, (z // 4 * 4 + x) * 2 + core

    def block_target(d):
        shift = (1, 2 - 4 * (zl % 2), -1)[d - 1]
        there_mode, there_cell = shifted_z(shift)
        return (
            (1 - core) * there_mode + core * on_scatter_axis((s + d) % 4),
            (1 - core) * there_cell + core * cell,
        )

    barrier = pltpu.get_barrier_semaphore()

    def greet(m, c):
        pl.semaphore_signal(barrier, 1, device_id=(m, c), device_id_type=MESH)

    for d in (1, 2, 3):
        greet(on_gather_axis((g + d) % 4), cell)
        greet(on_scatter_axis((s + d) % 4), cell)

    @pl.when(core == 0)
    def _():
        for shift in (1, -1, 2, -2):
            greet(*shifted_z(shift))

    @pl.when(cell > 0)
    def _():
        greet(mode, cell - 1)

    @pl.when(cell < 31)
    def _():
        greet(mode, cell + 1)

    loads = [
        pltpu.make_async_copy(pop_hbm, pop, load_sem.at[0]),
        pltpu.make_async_copy(mask_hbm, mask, load_sem.at[1]),
        pltpu.make_async_copy(octant_hbm, octant, load_sem.at[2]),
        pltpu.make_async_copy(courant_hbm, courant, load_sem.at[3]),
    ]
    for load in loads:
        load.start()

    def columns(place, i):
        return pl.ds(pl.multiple_of(((1 - core) * (place * 4 + i) + core * (i * 4 + place)) * B, B), B)

    own_blocks = [
        pltpu.make_async_copy(
            coll_hbm.at[:, columns(s, i)], blocks.at[s, :, pl.ds(i * B, B)], block_sem.at[i]
        )
        for i in range(4)
    ]
    for copy in own_blocks:
        copy.start()

    loads[0].wait()
    loads[1].wait()
    keep = (1 - mask[...]).astype(F32)
    keeps = [keep[r : r + 1, :] for r in (0, 1)]
    rows = pl.ds(pl.multiple_of(g * B, B), B)
    for r in (0, 1):
        first = keeps[r] * pop[pl.ds(r, B, stride=2), :]
        field[0, r] = first
        gathered[0, r, rows, :] = first.astype(BF16)

    @pl.when(cell == 0)
    def _():
        for stage in (0, 1):
            halo[stage, 0] = jnp.zeros((B, B), BF16)

    @pl.when(cell == 31)
    def _():
        for stage in (0, 1):
            halo[stage, 1] = jnp.zeros((B, B), BF16)

    pl.semaphore_wait(
        barrier,
        6 + 4 * (1 - core) + jnp.where(cell > 0, 1, 0) + jnp.where(cell < 31, 1, 0),
    )

    def gather_copy(stage, r, d):
        mine = gathered.at[stage, r, rows, :]
        return pltpu.make_async_remote_copy(
            mine, mine, gather_send.at[stage, r, d - 1], gather_recv.at[stage, r, d - 1],
            device_id=(on_gather_axis((g + d) % 4), cell), device_id_type=MESH,
        )

    def halo_copy(stage, side):
        return pltpu.make_async_remote_copy(
            gathered.at[stage, 1 - side, rows, :], halo.at[stage, side],
            halo_send.at[stage, side], halo_recv.at[stage, side],
            device_id=(mode, jnp.where(side == 0, jnp.minimum(cell + 1, 31), jnp.maximum(cell - 1, 0))), device_id_type=MESH,
        )

    def block_copies(d):
        m, c = block_target(d)
        return [
            pltpu.make_async_remote_copy(
                coll_hbm.at[:, columns((s + d) % 4, i)], blocks.at[s, :, pl.ds(i * B, B)],
                blocks_send.at[d - 1, i], blocks_recv.at[d - 1, i],
                device_id=(m, c), device_id_type=MESH,
            )
            for i in range(4)
        ]

    def part_copy(stage, r, d):
        return pltpu.make_async_remote_copy(
            outgoing.at[stage, r, d - 1], incoming.at[stage, r, d - 1],
            part_send.at[stage, r, d - 1], part_recv.at[stage, r, d - 1],
            device_id=(on_scatter_axis((s + d) % 4), cell), device_id_type=MESH,
        )

    def send_halo(stage):
        @pl.when(cell < 31)
        def _():
            halo_copy(stage, 0).start()

        @pl.when(cell > 0)
        def _():
            halo_copy(stage, 1).start()

    def wait_halo(stage):
        @pl.when(cell > 0)
        def _():
            halo_copy(stage, 0).wait_recv()

        @pl.when(cell < 31)
        def _():
            halo_copy(stage, 1).wait_recv()

    for r in (0, 1):
        for d in (2, 1, 3):
            gather_copy(0, r, d).start()
    for d in (2, 1, 3):
        for copy in block_copies(d):
            copy.start()
    send_halo(0)

    loads[2].wait()
    loads[3].wait()
    signs = octant[...]
    total = None
    for axis in range(3):
        bit = (signs // (2**axis)) % 2
        v = (1.0 - 2.0 * bit.astype(F32)) * courant[axis : axis + 1, :]
        v = jnp.transpose(jnp.broadcast_to(v, (B, B)))
        up, down = jnp.maximum(v, 0.0), jnp.minimum(v, 0.0)
        if axis < 2:
            speed[2 * axis] = up
            speed[2 * axis + 1] = down
        total = up - down if total is None else total + (up - down)
    speed[4] = total

    def advected(stage, r):
        f = field[stage, r]
        low = field[stage, 0] if r == 1 else halo[stage, 0].astype(F32)
        high = field[stage, 1] if r == 0 else halo[stage, 1].astype(F32)
        adv = speed[4] * f - speed[0] * pltpu.roll(f, 1, 1) + speed[1] * pltpu.roll(f, B - 1, 1)
        return f - (adv - speed[2] * low + speed[3] * high)

    for stage in (0, 1):
        if stage == 0:
            for copy in own_blocks:
                copy.wait()
        for r in (0, 1):
            for d in (1, 2, 3):
                gather_copy(stage, r, d).wait_recv()
            q = gathered[stage, r]
            for d in (2, 1, 3):
                if stage == 0 and r == 0:
                    for copy in block_copies(4 - d):
                        copy.wait_recv()
                part = jnp.dot(blocks[(s + d) % 4], q, preferred_element_type=F32)
                outgoing[stage, r, d - 1] = part.astype(BF16)
                part_copy(stage, r, d).start()
            sums[r] = jnp.dot(blocks[s], q, preferred_element_type=F32)
        wait_halo(stage)
        for r in (0, 1):
            sums[r] = advected(stage, r) - sums[r]
        for r in (0, 1):
            for d in (1, 2, 3):
                part_copy(stage, r, d).wait_recv()
            rest = incoming[stage, r, 0].astype(F32) + incoming[stage, r, 1].astype(F32) + incoming[stage, r, 2].astype(F32)
            if stage == 0:
                second = keeps[r] * (sums[r] - rest)
                field[1, r] = second
                gathered[1, r, rows, :] = second.astype(BF16)
                for d in (2, 1, 3):
                    gather_copy(1, r, d).start()
            else:
                out_ref[pl.ds(r, B, stride=2), :] = keeps[r] * (0.5 * field[0, r] + 0.5 * (sums[r] - rest))
        if stage == 0:
            send_halo(1)

    for d in (1, 2, 3):
        for copy in block_copies(d):
            copy.wait_send()
    for stage in (0, 1):
        for r in (0, 1):
            for d in (1, 2, 3):
                gather_copy(stage, r, d).wait_send()
                part_copy(stage, r, d).wait_send()

        @pl.when(cell < 31)
        def _():
            halo_copy(stage, 0).wait_send()

        @pl.when(cell > 0)
        def _():
            halo_copy(stage, 1).wait_send()


def on_device(populations, contact_mask, octant, courant, collision):
    dma = pltpu.SemaphoreType.DMA
    out = pl.pallas_call(
        kernel,
        out_shape=jax.ShapeDtypeStruct((2 * B, B), F32),
        in_specs=[pl.BlockSpec(memory_space=pl.ANY)] * 5,
        out_specs=pl.BlockSpec(memory_space=pltpu.VMEM),
        scratch_shapes=[
            pltpu.VMEM((2 * B, B), F32),
            pltpu.VMEM((2, B), jnp.int32),
            pltpu.VMEM((1, B), jnp.int32),
            pltpu.VMEM((3, B), F32),
            pltpu.VMEM((5, B, B), F32),
            pltpu.VMEM((4, B, 4 * B), BF16),
            pltpu.VMEM((2, 2, 4 * B, B), BF16),
            pltpu.VMEM((2, 2, B, B), BF16),
            pltpu.VMEM((2, B, B), F32),
            pltpu.VMEM((2, 2, 3, B, B), BF16),
            pltpu.VMEM((2, 2, 3, B, B), BF16),
            pltpu.VMEM((2, 2, B, B), F32),
            dma((4,)),
            dma((4,)),
            dma((3, 4)),
            dma((3, 4)),
            dma((2, 2, 3)),
            dma((2, 2, 3)),
            dma((2, 2)),
            dma((2, 2)),
            dma((2, 2, 3)),
            dma((2, 2, 3)),
        ],
        compiler_params=pltpu.CompilerParams(collective_id=0, has_side_effects=True),
        name="heun",
    )(
        populations.reshape(2 * B, B),
        contact_mask.reshape(2, B),
        octant.reshape(1, B),
        courant,
        collision,
    )
    return out.reshape(populations.shape)


def solution(mesh):
    placed = (
        P("mode", None, "cell", None),
        P(None, "cell", None),
        P("mode"),
        P(None, "mode"),
        P("mode", None),
    )
    return jax.shard_map(
        on_device,
        mesh=mesh,
        in_specs=placed,
        out_specs=P("mode", None, "cell", None),
        check_vma=False,
    )
```

```python
import jax
import jax.numpy as jnp
from jax import lax
from jax.experimental import pallas as pl
from jax.experimental.pallas import tpu as pltpu
from jax.sharding import PartitionSpec as P


B = 128
MESH = pl.DeviceIdType.MESH
F32, BF16 = jnp.float32, jnp.bfloat16


def kernel(
    pop_hbm, mask_hbm, octant_hbm, courant_hbm, coll_hbm, out_ref,
    pop, mask, octant, courant, speed, blocks, gathered, halo, sums, outgoing, incoming, field,
    load_sem, block_sem, blocks_send, blocks_recv, gather_send, gather_recv, halo_send, halo_recv, part_send, part_recv, far_sem, ready_sem,
):
    mode, cell = lax.axis_index("mode"), lax.axis_index("cell")
    y, zl = mode % 4, mode // 4
    hw_core, x, zh = cell % 2, cell // 2 % 4, cell // 8
    core = 1 - hw_core
    g = (1 - core) * y + core * zl
    s = (1 - core) * zl + core * y

    def on_gather_axis(place):
        return (1 - core) * (zl * 4 + place) + core * (place * 4 + y)

    def on_scatter_axis(place):
        return (1 - core) * (place * 4 + y) + core * (zl * 4 + place)

    def shifted_z(shift):
        z = (zh * 4 + zl + shift + 16) % 16
        return z % 4 * 4 + y, (z // 4 * 4 + x) * 2 + hw_core

    def block_target(d):
        shift = (1, 2 - 4 * (zl // 2), -1)[d - 1]
        there_mode, there_cell = shifted_z(shift)
        return (
            (1 - core) * there_mode + core * on_scatter_axis((s + d) % 4),
            (1 - core) * there_cell + core * cell,
        )

    barrier = pltpu.get_barrier_semaphore()

    def greet(m, c):
        pl.semaphore_signal(barrier, 1, device_id=(m, c), device_id_type=MESH)

    late = ((cell % 8 == 7) & (zh == 2)) | ((cell % 8 == 0) & ((zh == 1) | (zh == 2)))
    early = ((cell % 8 == 7) & (zh < 2)) | ((cell % 8 == 0) & (zh == 3))
    ordered = late
    partners = []
    for d in (1, 2, 3):
        for there in (on_gather_axis((g + d) % 4), on_scatter_axis((s + d) % 4)):
            partners.append(there)

            @pl.when(jnp.logical_not(ordered) | (there > mode))
            def _(there=there):
                greet(there, cell)

    @pl.when(core == 0)
    def _():
        for shift in (1, -1):
            greet(*shifted_z(shift))

    far_next = (cell % 8 == 7) & (cell < 31)
    far_back = (cell % 8 == 0) & (cell > 0)

    @pl.when((cell > 0) & jnp.logical_not(far_back & late))
    def _():
        greet(mode, cell - 1)

    @pl.when((cell < 31) & jnp.logical_not(far_next & late))
    def _():
        greet(mode, cell + 1)

    loads = [
        pltpu.make_async_copy(pop_hbm, pop, load_sem.at[0]),
        pltpu.make_async_copy(mask_hbm, mask, load_sem.at[1]),
        pltpu.make_async_copy(octant_hbm, octant, load_sem.at[2]),
        pltpu.make_async_copy(courant_hbm, courant, load_sem.at[3]),
    ]
    for load in loads:
        load.start()

    def columns(place, i):
        return pl.ds(pl.multiple_of(((1 - core) * (place * 4 + i) + core * (i * 4 + place)) * B, B), B)

    own_blocks = [
        pltpu.make_async_copy(
            coll_hbm.at[:, columns(s, i)], blocks.at[s, :, pl.ds(i * B, B)], block_sem.at[i]
        )
        for i in range(4)
    ]
    for copy in own_blocks:
        copy.start()

    loads[0].wait()
    loads[1].wait()
    keep = (1 - mask[...]).astype(F32)
    keeps = [keep[r : r + 1, :] for r in (0, 1)]
    rows = pl.ds(pl.multiple_of(g * B, B), B)
    for r in (0, 1):
        first = keeps[r] * pop[pl.ds(r, B, stride=2), :]
        field[0, r] = first
        gathered[0, r, rows, :] = first.astype(BF16)

    @pl.when(cell == 0)
    def _():
        for stage in (0, 1):
            halo[stage, 0] = jnp.zeros((B, B), BF16)

    @pl.when(cell == 31)
    def _():
        for stage in (0, 1):
            halo[stage, 1] = jnp.zeros((B, B), BF16)

    pl.semaphore_wait(
        barrier,
        jnp.where(ordered, g + s, 6) + 2 * (1 - core) + jnp.where(cell > 0, 1, 0) + jnp.where(cell < 31, 1, 0) - jnp.where(early, 1, 0),
    )

    @pl.when(late)
    def _():
        pl.semaphore_signal(far_sem, 1, device_id=(mode, jnp.where(far_next, cell + 1, cell - 1)), device_id_type=MESH)

    for there in partners:

        @pl.when(ordered & (there < mode))
        def _(there=there):
            pl.semaphore_signal(ready_sem, 1, device_id=(there, cell), device_id_type=MESH)

    def gather_copy(stage, r, d):
        mine = gathered.at[stage, r, rows, :]
        return pltpu.make_async_remote_copy(
            mine, mine, gather_send.at[stage, r, d - 1], gather_recv.at[stage, r, d - 1],
            device_id=(on_gather_axis((g + d) % 4), cell), device_id_type=MESH,
        )

    def halo_copy(stage, side):
        return pltpu.make_async_remote_copy(
            gathered.at[stage, 1 - side, rows, :], halo.at[stage, side],
            halo_send.at[stage, side], halo_recv.at[stage, side],
            device_id=(mode, jnp.where(side == 0, jnp.minimum(cell + 1, 31), jnp.maximum(cell - 1, 0))), device_id_type=MESH,
        )

    def block_copies(d):
        m, c = block_target(d)
        return [
            pltpu.make_async_remote_copy(
                coll_hbm.at[:, columns((s + d) % 4, i)], blocks.at[s, :, pl.ds(i * B, B)],
                blocks_send.at[d - 1, i], blocks_recv.at[d - 1, i],
                device_id=(m, c), device_id_type=MESH,
            )
            for i in range(4)
        ]

    def part_copy(stage, r, d):
        return pltpu.make_async_remote_copy(
            outgoing.at[stage, r, d - 1], incoming.at[stage, r, d - 1],
            part_send.at[stage, r, d - 1], part_recv.at[stage, r, d - 1],
            device_id=(on_scatter_axis((s + d) % 4), cell), device_id_type=MESH,
        )

    def send_halo(stage):
        @pl.when((cell < 31) & (jnp.logical_not(far_next) if stage == 0 else True))
        def _():
            halo_copy(stage, 0).start()

        @pl.when((cell > 0) & (jnp.logical_not(far_back) if stage == 0 else True))
        def _():
            halo_copy(stage, 1).start()

    def wait_halo(stage):
        @pl.when(cell > 0)
        def _():
            halo_copy(stage, 0).wait_recv()

        @pl.when(cell < 31)
        def _():
            halo_copy(stage, 1).wait_recv()

    def send_far():
        @pl.when(far_next)
        def _():
            halo_copy(0, 0).start()

        @pl.when(far_back)
        def _():
            halo_copy(0, 1).start()

    pl.when(late)(send_far)

    for later in (False, True):
        for r in (0, 1):
            for d in (2, 1, 3):

                @pl.when((jnp.logical_not(ordered) | (on_gather_axis((g + d) % 4) > mode)) == later)
                def _(r=r, d=d):
                    gather_copy(0, r, d).start()

        if not later:

            @pl.when(ordered & (g + s < 6))
            def _():
                pl.semaphore_wait(ready_sem, 6 - g - s)

    for d in (2, 1, 3):
        for copy in block_copies(d):
            copy.start()
    send_halo(0)

    @pl.when(early)
    def _():
        pl.semaphore_wait(far_sem, 1)
        send_far()

    loads[2].wait()
    loads[3].wait()
    signs = octant[...]
    total = None
    for axis in range(3):
        bit = (signs // (2**axis)) % 2
        v = (1.0 - 2.0 * bit.astype(F32)) * courant[axis : axis + 1, :]
        v = jnp.transpose(jnp.broadcast_to(v, (B, B)))
        up, down = jnp.maximum(v, 0.0), jnp.minimum(v, 0.0)
        if axis < 2:
            speed[2 * axis] = up
            speed[2 * axis + 1] = down
        total = up - down if total is None else total + (up - down)
    speed[4] = total

    def advected(stage, r):
        f = field[stage, r]
        low = field[stage, 0] if r == 1 else halo[stage, 0].astype(F32)
        high = field[stage, 1] if r == 0 else halo[stage, 1].astype(F32)
        adv = speed[4] * f - speed[0] * pltpu.roll(f, 1, 1) + speed[1] * pltpu.roll(f, B - 1, 1)
        return f - (adv - speed[2] * low + speed[3] * high)

    for stage in (0, 1):
        if stage == 0:
            for copy in own_blocks:
                copy.wait()
        for r in (0, 1):
            for d in (1, 2, 3):
                gather_copy(stage, r, d).wait_recv()
            q = gathered[stage, r]
            for d in (2, 1, 3):
                if stage == 0 and r == 0:
                    for copy in block_copies(4 - d):
                        copy.wait_recv()
                part = jnp.dot(blocks[(s + d) % 4], q, preferred_element_type=F32)
                outgoing[stage, r, d - 1] = part.astype(BF16)
                part_copy(stage, r, d).start()
            sums[r] = jnp.dot(blocks[s], q, preferred_element_type=F32)
        wait_halo(stage)
        for r in (0, 1):
            sums[r] = advected(stage, r) - sums[r]
        for r in (0, 1):
            for d in (1, 2, 3):
                part_copy(stage, r, d).wait_recv()
            rest = incoming[stage, r, 0].astype(F32) + incoming[stage, r, 1].astype(F32) + incoming[stage, r, 2].astype(F32)
            if stage == 0:
                second = keeps[r] * (sums[r] - rest)
                field[1, r] = second
                gathered[1, r, rows, :] = second.astype(BF16)
                for d in (2, 1, 3):
                    gather_copy(1, r, d).start()
            else:
                out_ref[pl.ds(r, B, stride=2), :] = keeps[r] * (0.5 * field[0, r] + 0.5 * (sums[r] - rest))
        if stage == 0:
            send_halo(1)

    for d in (1, 2, 3):
        for copy in block_copies(d):
            copy.wait_send()
    for stage in (0, 1):
        for r in (0, 1):
            for d in (1, 2, 3):
                gather_copy(stage, r, d).wait_send()
                part_copy(stage, r, d).wait_send()

        @pl.when(cell < 31)
        def _():
            halo_copy(stage, 0).wait_send()

        @pl.when(cell > 0)
        def _():
            halo_copy(stage, 1).wait_send()


def on_device(populations, contact_mask, octant, courant, collision):
    dma = pltpu.SemaphoreType.DMA
    out = pl.pallas_call(
        kernel,
        out_shape=pltpu.VMEM((2 * B, B), F32),
        in_specs=[pl.BlockSpec(memory_space=pl.ANY)] * 5,
        out_specs=pl.BlockSpec(memory_space=pltpu.VMEM),
        scratch_shapes=[
            pltpu.VMEM((2 * B, B), F32),
            pltpu.VMEM((2, B), jnp.int32),
            pltpu.VMEM((1, B), jnp.int32),
            pltpu.VMEM((3, B), F32),
            pltpu.VMEM((5, B, B), F32),
            pltpu.VMEM((4, B, 4 * B), BF16),
            pltpu.VMEM((2, 2, 4 * B, B), BF16),
            pltpu.VMEM((2, 2, B, B), BF16),
            pltpu.VMEM((2, B, B), F32),
            pltpu.VMEM((2, 2, 3, B, B), BF16),
            pltpu.VMEM((2, 2, 3, B, B), BF16),
            pltpu.VMEM((2, 2, B, B), F32),
            dma((4,)),
            dma((4,)),
            dma((3, 4)),
            dma((3, 4)),
            dma((2, 2, 3)),
            dma((2, 2, 3)),
            dma((2, 2)),
            dma((2, 2)),
            dma((2, 2, 3)),
            dma((2, 2, 3)),
            pltpu.SemaphoreType.REGULAR,
            pltpu.SemaphoreType.REGULAR,
        ],
        compiler_params=pltpu.CompilerParams(collective_id=0, has_side_effects=True),
        name="heun",
    )(
        populations.reshape(2 * B, B),
        contact_mask.reshape(2, B),
        octant.reshape(1, B),
        courant,
        collision,
    )
    return out.reshape(populations.shape)


def solution(mesh):
    placed = (
        P("mode", None, "cell", None),
        P(None, "cell", None),
        P("mode"),
        P(None, "mode"),
        P("mode", None),
    )
    return jax.shard_map(
        on_device,
        mesh=mesh,
        in_specs=placed,
        out_specs=P("mode", None, "cell", None),
        check_vma=False,
    )
```

```python
import jax
import jax.numpy as jnp
from jax import lax
from jax.experimental import pallas as pl
from jax.experimental.pallas import tpu as pltpu
from jax.sharding import PartitionSpec as P


B = 128
MESH = pl.DeviceIdType.MESH
F32, BF16 = jnp.float32, jnp.bfloat16


def kernel(
    pop_hbm, mask_hbm, octant_hbm, courant_hbm, coll_hbm, out_ref,
    pop, mask, octant, courant, speed, blocks, gathered, halo, sums, outgoing, incoming, field,
    load_sem, block_sem, blocks_send, blocks_recv, gather_send, gather_recv, halo_send, halo_recv, part_send, part_recv, far_sem, ready_sem,
):
    mode, cell = lax.axis_index("mode"), lax.axis_index("cell")
    y, zl = mode % 4, mode // 4
    hw_core, x, zh = cell % 2, cell // 2 % 4, cell // 8
    core = 1 - hw_core
    g = (1 - core) * y + core * zl
    s = (1 - core) * zl + core * y

    def on_gather_axis(place):
        return (1 - core) * (zl * 4 + place) + core * (place * 4 + y)

    def on_scatter_axis(place):
        return (1 - core) * (place * 4 + y) + core * (zl * 4 + place)

    def shifted_z(shift):
        z = (zh * 4 + zl + shift + 16) % 16
        return z % 4 * 4 + y, (z // 4 * 4 + x) * 2 + hw_core

    def block_target(d):
        shift = (1, 2 - 4 * (zl // 2), -1)[d - 1]
        there_mode, there_cell = shifted_z(shift)
        return (
            (1 - core) * there_mode + core * on_scatter_axis((s + d) % 4),
            (1 - core) * there_cell + core * cell,
        )

    barrier = pltpu.get_barrier_semaphore()

    def greet(m, c):
        pl.semaphore_signal(barrier, 1, device_id=(m, c), device_id_type=MESH)

    late = ((cell % 8 == 7) & (zh == 2)) | ((cell % 8 == 0) & ((zh == 1) | (zh == 2)))
    early = ((cell % 8 == 7) & (zh < 2)) | ((cell % 8 == 0) & (zh == 3))
    ordered = late
    partners = []
    for d in (1, 2, 3):
        for there in (on_gather_axis((g + d) % 4), on_scatter_axis((s + d) % 4)):
            partners.append(there)

            @pl.when(jnp.logical_not(ordered) | (there > mode))
            def _(there=there):
                greet(there, cell)

    @pl.when(core == 0)
    def _():
        for shift in (1, -1):
            greet(*shifted_z(shift))

    far_next = (cell % 8 == 7) & (cell < 31)
    far_back = (cell % 8 == 0) & (cell > 0)

    @pl.when((cell > 0) & jnp.logical_not(far_back & late))
    def _():
        greet(mode, cell - 1)

    @pl.when((cell < 31) & jnp.logical_not(far_next & late))
    def _():
        greet(mode, cell + 1)

    loads = [
        pltpu.make_async_copy(pop_hbm, pop, load_sem.at[0]),
        pltpu.make_async_copy(mask_hbm, mask, load_sem.at[1]),
        pltpu.make_async_copy(octant_hbm, octant, load_sem.at[2]),
        pltpu.make_async_copy(courant_hbm, courant, load_sem.at[3]),
    ]
    for load in loads:
        load.start()

    def columns(place, i):
        return pl.ds(pl.multiple_of(((1 - core) * (place * 4 + i) + core * (i * 4 + place)) * B, B), B)

    own_blocks = [
        pltpu.make_async_copy(
            coll_hbm.at[:, columns(s, i)], blocks.at[s, :, pl.ds(i * B, B)], block_sem.at[i]
        )
        for i in range(4)
    ]
    for copy in own_blocks:
        copy.start()

    loads[0].wait()
    loads[1].wait()
    keep = (1 - mask[...]).astype(F32)
    keeps = [keep[r : r + 1, :] for r in (0, 1)]
    rows = pl.ds(pl.multiple_of(g * B, B), B)
    for r in (0, 1):
        first = keeps[r] * pop[pl.ds(r, B, stride=2), :]
        field[0, r] = first
        gathered[0, r, rows, :] = first.astype(BF16)

    @pl.when(cell == 0)
    def _():
        for stage in (0, 1):
            halo[stage, 0] = jnp.zeros((B, B), BF16)

    @pl.when(cell == 31)
    def _():
        for stage in (0, 1):
            halo[stage, 1] = jnp.zeros((B, B), BF16)

    pl.semaphore_wait(
        barrier,
        jnp.where(ordered, g + s, 6) + 2 * (1 - core) + jnp.where(cell > 0, 1, 0) + jnp.where(cell < 31, 1, 0) - jnp.where(early, 1, 0),
    )

    @pl.when(late)
    def _():
        pl.semaphore_signal(far_sem, 1, device_id=(mode, jnp.where(far_next, cell + 1, cell - 1)), device_id_type=MESH)

    for there in partners:

        @pl.when(ordered & (there < mode))
        def _(there=there):
            pl.semaphore_signal(ready_sem, 1, device_id=(there, cell), device_id_type=MESH)

    def gather_copy(stage, r, d):
        mine = gathered.at[stage, r, rows, :]
        return pltpu.make_async_remote_copy(
            mine, mine, gather_send.at[stage, r, d - 1], gather_recv.at[stage, r, d - 1],
            device_id=(on_gather_axis((g + d) % 4), cell), device_id_type=MESH,
        )

    def halo_copy(stage, side):
        return pltpu.make_async_remote_copy(
            gathered.at[stage, 1 - side, rows, :], halo.at[stage, side],
            halo_send.at[stage, side], halo_recv.at[stage, side],
            device_id=(mode, jnp.where(side == 0, jnp.minimum(cell + 1, 31), jnp.maximum(cell - 1, 0))), device_id_type=MESH,
        )

    def block_copies(d):
        m, c = block_target(d)
        return [
            pltpu.make_async_remote_copy(
                coll_hbm.at[:, columns((s + d) % 4, i)], blocks.at[s, :, pl.ds(i * B, B)],
                blocks_send.at[d - 1, i], blocks_recv.at[d - 1, i],
                device_id=(m, c), device_id_type=MESH,
            )
            for i in range(4)
        ]

    def part_copy(stage, r, d):
        return pltpu.make_async_remote_copy(
            outgoing.at[stage, r, d - 1], incoming.at[stage, r, d - 1],
            part_send.at[stage, r, d - 1], part_recv.at[stage, r, d - 1],
            device_id=(on_scatter_axis((s + d) % 4), cell), device_id_type=MESH,
        )

    def send_halo(stage):
        @pl.when((cell < 31) & (jnp.logical_not(far_next) if stage == 0 else True))
        def _():
            halo_copy(stage, 0).start()

        @pl.when((cell > 0) & (jnp.logical_not(far_back) if stage == 0 else True))
        def _():
            halo_copy(stage, 1).start()

    def send_halo_row(r):
        @pl.when(cell < 31 if r else cell > 0)
        def _():
            halo_copy(1, 1 - r).start()

    def wait_halo(stage):
        @pl.when(cell > 0)
        def _():
            halo_copy(stage, 0).wait_recv()

        @pl.when(cell < 31)
        def _():
            halo_copy(stage, 1).wait_recv()

    def send_far():
        @pl.when(far_next)
        def _():
            halo_copy(0, 0).start()

        @pl.when(far_back)
        def _():
            halo_copy(0, 1).start()

    pl.when(late)(send_far)

    for later in (False, True):
        for r in (0, 1):
            for d in (2, 1, 3):

                @pl.when((jnp.logical_not(ordered) | (on_gather_axis((g + d) % 4) > mode)) == later)
                def _(r=r, d=d):
                    gather_copy(0, r, d).start()

        if not later:

            @pl.when(ordered & (g + s < 6))
            def _():
                pl.semaphore_wait(ready_sem, 6 - g - s)

    for d in (2, 1, 3):
        for copy in block_copies(d):
            copy.start()
    send_halo(0)

    @pl.when(early)
    def _():
        pl.semaphore_wait(far_sem, 1)
        send_far()

    loads[2].wait()
    loads[3].wait()
    signs = octant[...]
    total = None
    for axis in range(3):
        bit = (signs // (2**axis)) % 2
        v = (1.0 - 2.0 * bit.astype(F32)) * courant[axis : axis + 1, :]
        v = jnp.transpose(jnp.broadcast_to(v, (B, B)))
        up, down = jnp.maximum(v, 0.0), jnp.minimum(v, 0.0)
        if axis < 2:
            speed[2 * axis] = up
            speed[2 * axis + 1] = down
        total = up - down if total is None else total + (up - down)
    speed[4] = total

    def advected(stage, r):
        f = field[stage, r]
        low = field[stage, 0] if r == 1 else halo[stage, 0].astype(F32)
        high = field[stage, 1] if r == 0 else halo[stage, 1].astype(F32)
        adv = speed[4] * f - speed[0] * pltpu.roll(f, 1, 1) + speed[1] * pltpu.roll(f, B - 1, 1)
        return f - (adv - speed[2] * low + speed[3] * high)

    for stage in (0, 1):
        if stage == 0:
            for copy in own_blocks:
                copy.wait()
        for r in (0, 1):
            for d in (1, 2, 3):
                gather_copy(stage, r, d).wait_recv()
            q = gathered[stage, r]
            for d in (2, 1, 3):
                if stage == 0 and r == 0:
                    for copy in block_copies(4 - d):
                        copy.wait_recv()
                part = jnp.dot(blocks[(s + d) % 4], q, preferred_element_type=F32)
                outgoing[stage, r, d - 1] = part.astype(BF16)
                part_copy(stage, r, d).start()
            sums[r] = jnp.dot(blocks[s], q, preferred_element_type=F32)
        wait_halo(stage)
        for r in (0, 1):
            sums[r] = advected(stage, r) - sums[r]
        for r in (0, 1):
            for d in (1, 2, 3):
                part_copy(stage, r, d).wait_recv()
            rest = incoming[stage, r, 0].astype(F32) + incoming[stage, r, 1].astype(F32) + incoming[stage, r, 2].astype(F32)
            if stage == 0:
                second = keeps[r] * (sums[r] - rest)
                field[1, r] = second
                gathered[1, r, rows, :] = second.astype(BF16)
                for d in (2, 1, 3):
                    gather_copy(1, r, d).start()
                send_halo_row(r)
            else:
                out_ref[pl.ds(r, B, stride=2), :] = keeps[r] * (0.5 * field[0, r] + 0.5 * (sums[r] - rest))

    for d in (1, 2, 3):
        for copy in block_copies(d):
            copy.wait_send()
    for stage in (0, 1):
        for r in (0, 1):
            for d in (1, 2, 3):
                gather_copy(stage, r, d).wait_send()
                part_copy(stage, r, d).wait_send()

        @pl.when(cell < 31)
        def _():
            halo_copy(stage, 0).wait_send()

        @pl.when(cell > 0)
        def _():
            halo_copy(stage, 1).wait_send()


def on_device(populations, contact_mask, octant, courant, collision):
    dma = pltpu.SemaphoreType.DMA
    out = pl.pallas_call(
        kernel,
        out_shape=pltpu.VMEM((2 * B, B), F32),
        in_specs=[pl.BlockSpec(memory_space=pl.ANY)] * 5,
        out_specs=pl.BlockSpec(memory_space=pltpu.VMEM),
        scratch_shapes=[
            pltpu.VMEM((2 * B, B), F32),
            pltpu.VMEM((2, B), jnp.int32),
            pltpu.VMEM((1, B), jnp.int32),
            pltpu.VMEM((3, B), F32),
            pltpu.VMEM((5, B, B), F32),
            pltpu.VMEM((4, B, 4 * B), BF16),
            pltpu.VMEM((2, 2, 4 * B, B), BF16),
            pltpu.VMEM((2, 2, B, B), BF16),
            pltpu.VMEM((2, B, B), F32),
            pltpu.VMEM((2, 2, 3, B, B), BF16),
            pltpu.VMEM((2, 2, 3, B, B), BF16),
            pltpu.VMEM((2, 2, B, B), F32),
            dma((4,)),
            dma((4,)),
            dma((3, 4)),
            dma((3, 4)),
            dma((2, 2, 3)),
            dma((2, 2, 3)),
            dma((2, 2)),
            dma((2, 2)),
            dma((2, 2, 3)),
            dma((2, 2, 3)),
            pltpu.SemaphoreType.REGULAR,
            pltpu.SemaphoreType.REGULAR,
        ],
        compiler_params=pltpu.CompilerParams(collective_id=0, has_side_effects=True),
        name="heun",
    )(
        populations.reshape(2 * B, B),
        contact_mask.reshape(2, B),
        octant.reshape(1, B),
        courant,
        collision,
    )
    return out.reshape(populations.shape)


def solution(mesh):
    placed = (
        P("mode", None, "cell", None),
        P(None, "cell", None),
        P("mode"),
        P(None, "mode"),
        P("mode", None),
    )
    return jax.shard_map(
        on_device,
        mesh=mesh,
        in_specs=placed,
        out_specs=P("mode", None, "cell", None),
        check_vma=False,
    )
```

```python
import jax
import jax.numpy as jnp
from jax import lax
from jax.experimental import pallas as pl
from jax.experimental.pallas import tpu as pltpu
from jax.sharding import PartitionSpec as P


B = 128
MESH = pl.DeviceIdType.MESH
F32, BF16 = jnp.float32, jnp.bfloat16


def kernel(
    pop_hbm, mask_hbm, octant_hbm, courant_hbm, coll_hbm, out_ref,
    pop, mask, octant, courant, speed, blocks, gathered, halo, sums, outgoing, incoming, field,
    load_sem, block_sem, blocks_send, blocks_recv, gather_send, gather_recv, halo_send, halo_recv, part_send, part_recv, far_sem,
):
    mode, cell = lax.axis_index("mode"), lax.axis_index("cell")
    y, zl = mode % 4, mode // 4
    hw_core, x, zh = cell % 2, cell // 2 % 4, cell // 8
    core = 1 - hw_core
    g = (1 - core) * y + core * zl
    s = (1 - core) * zl + core * y

    def on_gather_axis(place):
        return (1 - core) * (zl * 4 + place) + core * (place * 4 + y)

    def on_scatter_axis(place):
        return (1 - core) * (place * 4 + y) + core * (zl * 4 + place)

    def shifted_z(shift):
        z = (zh * 4 + zl + shift + 16) % 16
        return z % 4 * 4 + y, (z // 4 * 4 + x) * 2 + hw_core

    def block_target(d):
        shift = (1, 2 - 4 * (zl // 2), -1)[d - 1]
        there_mode, there_cell = shifted_z(shift)
        return (
            (1 - core) * there_mode + core * on_scatter_axis((s + d) % 4),
            (1 - core) * there_cell + core * cell,
        )

    barrier = pltpu.get_barrier_semaphore()

    def greet(m, c):
        pl.semaphore_signal(barrier, 1, device_id=(m, c), device_id_type=MESH)

    late = ((cell % 8 == 7) & (zh == 2)) | ((cell % 8 == 0) & ((zh == 1) | (zh == 2)))
    early = ((cell % 8 == 7) & (zh < 2)) | ((cell % 8 == 0) & (zh == 3))
    for d in (1, 2, 3):
        greet(on_gather_axis((g + d) % 4), cell)
        greet(on_scatter_axis((s + d) % 4), cell)

    @pl.when(core == 0)
    def _():
        for shift in (1, -1):
            greet(*shifted_z(shift))

    far_next = (cell % 8 == 7) & (cell < 31)
    far_back = (cell % 8 == 0) & (cell > 0)

    @pl.when((cell > 0) & jnp.logical_not(far_back & late))
    def _():
        greet(mode, cell - 1)

    @pl.when((cell < 31) & jnp.logical_not(far_next & late))
    def _():
        greet(mode, cell + 1)

    loads = [
        pltpu.make_async_copy(pop_hbm, pop, load_sem.at[0]),
        pltpu.make_async_copy(mask_hbm, mask, load_sem.at[1]),
        pltpu.make_async_copy(octant_hbm, octant, load_sem.at[2]),
        pltpu.make_async_copy(courant_hbm, courant, load_sem.at[3]),
    ]
    for load in loads:
        load.start()

    def columns(place, i):
        return pl.ds(pl.multiple_of(((1 - core) * (place * 4 + i) + core * (i * 4 + place)) * B, B), B)

    own_blocks = [
        pltpu.make_async_copy(
            coll_hbm.at[:, columns(s, i)], blocks.at[s, :, pl.ds(i * B, B)], block_sem.at[i]
        )
        for i in range(4)
    ]
    for copy in own_blocks:
        copy.start()

    loads[0].wait()
    loads[1].wait()
    keep = (1 - mask[...]).astype(F32)
    keeps = [keep[r : r + 1, :] for r in (0, 1)]
    rows = pl.ds(pl.multiple_of(g * B, B), B)
    for r in (0, 1):
        first = keeps[r] * pop[pl.ds(r, B, stride=2), :]
        field[0, r] = first
        gathered[0, r, rows, :] = first.astype(BF16)

    @pl.when(cell == 0)
    def _():
        for stage in (0, 1):
            halo[stage, 0] = jnp.zeros((B, B), BF16)

    @pl.when(cell == 31)
    def _():
        for stage in (0, 1):
            halo[stage, 1] = jnp.zeros((B, B), BF16)

    pl.semaphore_wait(
        barrier,
        6 + 2 * (1 - core) + jnp.where(cell > 0, 1, 0) + jnp.where(cell < 31, 1, 0) - jnp.where(early, 1, 0),
    )

    @pl.when(late)
    def _():
        pl.semaphore_signal(far_sem, 1, device_id=(mode, jnp.where(far_next, cell + 1, cell - 1)), device_id_type=MESH)

    def gather_copy(stage, r, d):
        mine = gathered.at[stage, r, rows, :]
        return pltpu.make_async_remote_copy(
            mine, mine, gather_send.at[stage, r, d - 1], gather_recv.at[stage, r, d - 1],
            device_id=(on_gather_axis((g + d) % 4), cell), device_id_type=MESH,
        )

    def halo_copy(stage, side):
        return pltpu.make_async_remote_copy(
            gathered.at[stage, 1 - side, rows, :], halo.at[stage, side],
            halo_send.at[stage, side], halo_recv.at[stage, side],
            device_id=(mode, jnp.where(side == 0, jnp.minimum(cell + 1, 31), jnp.maximum(cell - 1, 0))), device_id_type=MESH,
        )

    def block_copies(d):
        m, c = block_target(d)
        return [
            pltpu.make_async_remote_copy(
                coll_hbm.at[:, columns((s + d) % 4, i)], blocks.at[s, :, pl.ds(i * B, B)],
                blocks_send.at[d - 1, i], blocks_recv.at[d - 1, i],
                device_id=(m, c), device_id_type=MESH,
            )
            for i in range(4)
        ]

    def part_copy(stage, r, d):
        return pltpu.make_async_remote_copy(
            outgoing.at[stage, r, d - 1], incoming.at[stage, r, d - 1],
            part_send.at[stage, r, d - 1], part_recv.at[stage, r, d - 1],
            device_id=(on_scatter_axis((s + d) % 4), cell), device_id_type=MESH,
        )

    def send_halo(stage):
        @pl.when((cell < 31) & (jnp.logical_not(far_next) if stage == 0 else True))
        def _():
            halo_copy(stage, 0).start()

        @pl.when((cell > 0) & (jnp.logical_not(far_back) if stage == 0 else True))
        def _():
            halo_copy(stage, 1).start()

    def send_halo_row(r):
        @pl.when(cell < 31 if r else cell > 0)
        def _():
            halo_copy(1, 1 - r).start()

    def wait_halo(stage):
        @pl.when(cell > 0)
        def _():
            halo_copy(stage, 0).wait_recv()

        @pl.when(cell < 31)
        def _():
            halo_copy(stage, 1).wait_recv()

    def send_far():
        @pl.when(far_next)
        def _():
            halo_copy(0, 0).start()

        @pl.when(far_back)
        def _():
            halo_copy(0, 1).start()

    pl.when(late)(send_far)

    for r in (0, 1):
        for d in (2, 1, 3):
            gather_copy(0, r, d).start()
    send_halo(0)
    for d in (2, 1, 3):
        for copy in block_copies(d):
            copy.start()


    @pl.when(early)
    def _():
        pl.semaphore_wait(far_sem, 1)
        send_far()

    loads[2].wait()
    loads[3].wait()
    signs = octant[...]
    total = None
    for axis in range(3):
        bit = (signs // (2**axis)) % 2
        v = (1.0 - 2.0 * bit.astype(F32)) * courant[axis : axis + 1, :]
        v = jnp.transpose(jnp.broadcast_to(v, (B, B)))
        up, down = jnp.maximum(v, 0.0), jnp.minimum(v, 0.0)
        if axis < 2:
            speed[2 * axis] = up
            speed[2 * axis + 1] = down
        total = up - down if total is None else total + (up - down)
    speed[4] = total

    def advected(stage, r):
        f = field[stage, r]
        low = field[stage, 0] if r == 1 else halo[stage, 0].astype(F32)
        high = field[stage, 1] if r == 0 else halo[stage, 1].astype(F32)
        adv = speed[4] * f - speed[0] * pltpu.roll(f, 1, 1) + speed[1] * pltpu.roll(f, B - 1, 1)
        return f - (adv - speed[2] * low + speed[3] * high)

    for stage in (0, 1):
        if stage == 0:
            for copy in own_blocks:
                copy.wait()
        for r in (0, 1):
            for d in (1, 2, 3):
                gather_copy(stage, r, d).wait_recv()
            q = gathered[stage, r]
            for d in (2, 1, 3):
                if stage == 0 and r == 0:
                    for copy in block_copies(4 - d):
                        copy.wait_recv()
                part = jnp.dot(blocks[(s + d) % 4], q, preferred_element_type=F32)
                outgoing[stage, r, d - 1] = part.astype(BF16)
                part_copy(stage, r, d).start()
        for r in (0, 1):
            sums[r] = jnp.dot(blocks[s], gathered[stage, r], preferred_element_type=F32)
        wait_halo(stage)
        for r in (0, 1):
            sums[r] = advected(stage, r) - sums[r]
        for r in (0, 1):
            for d in (1, 2, 3):
                part_copy(stage, r, d).wait_recv()
            rest = incoming[stage, r, 0].astype(F32) + incoming[stage, r, 1].astype(F32) + incoming[stage, r, 2].astype(F32)
            if stage == 0:
                second = keeps[r] * (sums[r] - rest)
                field[1, r] = second
                gathered[1, r, rows, :] = second.astype(BF16)
                for d in (2, 1, 3):
                    gather_copy(1, r, d).start()
                send_halo_row(r)
            else:
                out_ref[pl.ds(r, B, stride=2), :] = keeps[r] * (0.5 * field[0, r] + 0.5 * (sums[r] - rest))

    for d in (1, 2, 3):
        for copy in block_copies(d):
            copy.wait_send()
    for stage in (0, 1):
        for r in (0, 1):
            for d in (1, 2, 3):
                gather_copy(stage, r, d).wait_send()
                part_copy(stage, r, d).wait_send()

        @pl.when(cell < 31)
        def _():
            halo_copy(stage, 0).wait_send()

        @pl.when(cell > 0)
        def _():
            halo_copy(stage, 1).wait_send()


def on_device(populations, contact_mask, octant, courant, collision):
    dma = pltpu.SemaphoreType.DMA
    out = pl.pallas_call(
        kernel,
        out_shape=pltpu.VMEM((2 * B, B), F32),
        in_specs=[pl.BlockSpec(memory_space=pl.ANY)] * 5,
        out_specs=pl.BlockSpec(memory_space=pltpu.VMEM),
        scratch_shapes=[
            pltpu.VMEM((2 * B, B), F32),
            pltpu.VMEM((2, B), jnp.int32),
            pltpu.VMEM((1, B), jnp.int32),
            pltpu.VMEM((3, B), F32),
            pltpu.VMEM((5, B, B), F32),
            pltpu.VMEM((4, B, 4 * B), BF16),
            pltpu.VMEM((2, 2, 4 * B, B), BF16),
            pltpu.VMEM((2, 2, B, B), BF16),
            pltpu.VMEM((2, B, B), F32),
            pltpu.VMEM((2, 2, 3, B, B), BF16),
            pltpu.VMEM((2, 2, 3, B, B), BF16),
            pltpu.VMEM((2, 2, B, B), F32),
            dma((4,)),
            dma((4,)),
            dma((3, 4)),
            dma((3, 4)),
            dma((2, 2, 3)),
            dma((2, 2, 3)),
            dma((2, 2)),
            dma((2, 2)),
            dma((2, 2, 3)),
            dma((2, 2, 3)),
            pltpu.SemaphoreType.REGULAR,
        ],
        compiler_params=pltpu.CompilerParams(collective_id=0, has_side_effects=True),
        name="heun",
    )(
        populations.reshape(2 * B, B),
        contact_mask.reshape(2, B),
        octant.reshape(1, B),
        courant,
        collision,
    )
    return out.reshape(populations.shape)


def solution(mesh):
    placed = (
        P("mode", None, "cell", None),
        P(None, "cell", None),
        P("mode"),
        P(None, "mode"),
        P("mode", None),
    )
    return jax.shard_map(
        on_device,
        mesh=mesh,
        in_specs=placed,
        out_specs=P("mode", None, "cell", None),
        check_vma=False,
    )
```

```python
import jax
import jax.numpy as jnp
from jax import lax
from jax.experimental import pallas as pl
from jax.experimental.pallas import tpu as pltpu
from jax.sharding import PartitionSpec as P


B = 128
MESH = pl.DeviceIdType.MESH
F32, BF16 = jnp.float32, jnp.bfloat16


def kernel(
    pop_hbm, mask_hbm, octant_hbm, courant_hbm, coll_hbm, out_ref,
    pop, mask, octant, courant, speed, blocks, gathered, halo, sums, outgoing, incoming, field,
    load_sem, block_sem, blocks_send, blocks_recv, gather_send, gather_recv, halo_send, halo_recv, part_send, part_recv, far_sem,
):
    mode, cell = lax.axis_index("mode"), lax.axis_index("cell")
    y, zl = mode % 4, mode // 4
    hw_core, x, zh = cell % 2, cell // 2 % 4, cell // 8
    core = 1 - hw_core
    g = (1 - core) * y + core * zl
    s = (1 - core) * zl + core * y

    def on_gather_axis(place):
        return (1 - core) * (zl * 4 + place) + core * (place * 4 + y)

    def on_scatter_axis(place):
        return (1 - core) * (place * 4 + y) + core * (zl * 4 + place)

    def shifted_z(shift):
        z = (zh * 4 + zl + shift + 16) % 16
        return z % 4 * 4 + y, (z // 4 * 4 + x) * 2 + hw_core

    def block_target(d):
        shift = (1, 2 - 4 * (zl // 2), -1)[d - 1]
        there_mode, there_cell = shifted_z(shift)
        return (
            (1 - core) * there_mode + core * on_scatter_axis((s + d) % 4),
            (1 - core) * there_cell + core * cell,
        )

    flip = jnp.where(cell == 16, 1, 0)

    barrier = pltpu.get_barrier_semaphore()

    def greet(m, c):
        pl.semaphore_signal(barrier, 1, device_id=(m, c), device_id_type=MESH)

    late = ((cell % 8 == 7) & (zh == 2)) | ((cell % 8 == 0) & ((zh == 1) | (zh == 2)))
    early = ((cell % 8 == 7) & (zh < 2)) | ((cell % 8 == 0) & (zh == 3))
    for d in (1, 2, 3):
        greet(on_gather_axis((g + d) % 4), cell)
        greet(on_scatter_axis((s + d) % 4), cell)

    @pl.when(core == 0)
    def _():
        for shift in (1, -1):
            greet(*shifted_z(shift))

    far_next = (cell % 8 == 7) & (cell < 31)
    far_back = (cell % 8 == 0) & (cell > 0)

    @pl.when((cell > 0) & jnp.logical_not(far_back & late))
    def _():
        greet(mode, cell - 1)

    @pl.when((cell < 31) & jnp.logical_not(far_next & late))
    def _():
        greet(mode, cell + 1)

    loads = [
        pltpu.make_async_copy(pop_hbm, pop, load_sem.at[0]),
        pltpu.make_async_copy(mask_hbm, mask, load_sem.at[1]),
        pltpu.make_async_copy(octant_hbm, octant, load_sem.at[2]),
        pltpu.make_async_copy(courant_hbm, courant, load_sem.at[3]),
    ]
    for load in loads:
        load.start()

    def columns(place, i):
        return pl.ds(pl.multiple_of(((1 - core) * (place * 4 + i) + core * (i * 4 + place)) * B, B), B)

    own_blocks = [
        pltpu.make_async_copy(
            coll_hbm.at[:, columns(s, i)], blocks.at[s, :, pl.ds(i * B, B)], block_sem.at[i]
        )
        for i in range(4)
    ]
    for copy in own_blocks:
        copy.start()

    loads[0].wait()
    loads[1].wait()
    keep = (1 - mask[...]).astype(F32)
    keeps = [keep[r : r + 1, :] for r in (0, 1)]
    rows = pl.ds(pl.multiple_of(g * B, B), B)
    for r in (0, 1):
        first = keeps[r] * pop[pl.ds(r, B, stride=2), :]
        field[0, r] = first
        gathered[0, r, rows, :] = first.astype(BF16)

    @pl.when(cell == 0)
    def _():
        for stage in (0, 1):
            halo[stage, 0] = jnp.zeros((B, B), BF16)

    @pl.when(cell == 31)
    def _():
        for stage in (0, 1):
            halo[stage, 1] = jnp.zeros((B, B), BF16)

    pl.semaphore_wait(
        barrier,
        6 + 2 * (1 - core) + jnp.where(cell > 0, 1, 0) + jnp.where(cell < 31, 1, 0) - jnp.where(early, 1, 0),
    )

    @pl.when(late)
    def _():
        pl.semaphore_signal(far_sem, 1, device_id=(mode, jnp.where(far_next, cell + 1, cell - 1)), device_id_type=MESH)

    def gather_copy(stage, r, d):
        mine = gathered.at[stage, r, rows, :]
        return pltpu.make_async_remote_copy(
            mine, mine, gather_send.at[stage, r, d - 1], gather_recv.at[stage, r, d - 1],
            device_id=(on_gather_axis((g + d) % 4), cell), device_id_type=MESH,
        )

    def halo_copy(stage, side):
        return pltpu.make_async_remote_copy(
            gathered.at[stage, 1 - side, rows, :], halo.at[stage, side],
            halo_send.at[stage, side], halo_recv.at[stage, side],
            device_id=(mode, jnp.where(side == 0, jnp.minimum(cell + 1, 31), jnp.maximum(cell - 1, 0))), device_id_type=MESH,
        )

    def block_copies(d):
        m, c = block_target(d)
        return [
            pltpu.make_async_remote_copy(
                coll_hbm.at[:, columns((s + d) % 4, i)], blocks.at[s, :, pl.ds(i * B, B)],
                blocks_send.at[d - 1, i], blocks_recv.at[d - 1, i],
                device_id=(m, c), device_id_type=MESH,
            )
            for i in range(4)
        ]

    def part_copy(stage, r, d):
        return pltpu.make_async_remote_copy(
            outgoing.at[stage, r, d - 1], incoming.at[stage, r, d - 1],
            part_send.at[stage, r, d - 1], part_recv.at[stage, r, d - 1],
            device_id=(on_scatter_axis((s + d) % 4), cell), device_id_type=MESH,
        )

    def send_halo(stage):
        @pl.when((cell < 31) & (jnp.logical_not(far_next) if stage == 0 else True))
        def _():
            halo_copy(stage, 0).start()

        @pl.when((cell > 0) & (jnp.logical_not(far_back) if stage == 0 else True))
        def _():
            halo_copy(stage, 1).start()

    def send_halo_row(r):
        @pl.when(cell < 31 if r else cell > 0)
        def _():
            halo_copy(1, 1 - r).start()

    def wait_halo(stage, side):
        @pl.when(cell < 31 if side else cell > 0)
        def _():
            halo_copy(stage, side).wait_recv()

    def send_far():
        @pl.when(far_next)
        def _():
            halo_copy(0, 0).start()

        @pl.when(far_back)
        def _():
            halo_copy(0, 1).start()

    pl.when(late)(send_far)

    for k in (0, 1):
        for d in (2, 1, 3):
            gather_copy(0, (k + flip) % 2, d).start()
    send_halo(0)
    for d in (2, 1, 3):
        for copy in block_copies(d):
            copy.start()


    @pl.when(early)
    def _():
        pl.semaphore_wait(far_sem, 1)
        send_far()

    loads[2].wait()
    loads[3].wait()
    signs = octant[...]
    total = None
    for axis in range(3):
        bit = (signs // (2**axis)) % 2
        v = (1.0 - 2.0 * bit.astype(F32)) * courant[axis : axis + 1, :]
        v = jnp.transpose(jnp.broadcast_to(v, (B, B)))
        up, down = jnp.maximum(v, 0.0), jnp.minimum(v, 0.0)
        if axis < 2:
            speed[2 * axis] = up
            speed[2 * axis + 1] = down
        total = up - down if total is None else total + (up - down)
    speed[4] = total

    def advected(stage, r):
        f = field[stage, r]
        low = field[stage, 0] if r == 1 else halo[stage, 0].astype(F32)
        high = field[stage, 1] if r == 0 else halo[stage, 1].astype(F32)
        adv = speed[4] * f - speed[0] * pltpu.roll(f, 1, 1) + speed[1] * pltpu.roll(f, B - 1, 1)
        return f - (adv - speed[2] * low + speed[3] * high)

    for stage in (0, 1):
        if stage == 0:
            for copy in own_blocks:
                copy.wait()
        for k in (0, 1):
            r = (k + flip) % 2
            for d in (1, 2, 3):
                gather_copy(stage, r, d).wait_recv()
            q = gathered[stage, r]
            for d in (2, 1, 3):
                if stage == 0 and k == 0:
                    for copy in block_copies(4 - d):
                        copy.wait_recv()
                part = jnp.dot(blocks[(s + d) % 4], q, preferred_element_type=F32)
                outgoing[stage, r, d - 1] = part.astype(BF16)
                part_copy(stage, r, d).start()
        for r in (0, 1):
            sums[r] = jnp.dot(blocks[s], gathered[stage, r], preferred_element_type=F32)

        def rest(stage, r):
            for d in (1, 2, 3):
                part_copy(stage, r, d).wait_recv()
            return incoming[stage, r, 0].astype(F32) + incoming[stage, r, 1].astype(F32) + incoming[stage, r, 2].astype(F32)

        def finish_first(r):
            wait_halo(0, r)
            base = advected(0, r) - sums[r]
            second = keeps[r] * (base - rest(0, r))
            field[1, r] = second
            gathered[1, r, rows, :] = second.astype(BF16)
            for d in (2, 1, 3):
                gather_copy(1, r, d).start()
            send_halo_row(r)

        if stage == 0:

            @pl.when(flip == 0)
            def _():
                finish_first(0)
                finish_first(1)

            @pl.when(flip == 1)
            def _():
                finish_first(1)
                finish_first(0)

        else:
            for r in (0, 1):
                wait_halo(1, r)
            for r in (0, 1):
                sums[r] = advected(1, r) - sums[r]
            for r in (0, 1):
                out_ref[pl.ds(r, B, stride=2), :] = keeps[r] * (0.5 * field[0, r] + 0.5 * (sums[r] - rest(1, r)))

    for d in (1, 2, 3):
        for copy in block_copies(d):
            copy.wait_send()
    for stage in (0, 1):
        for r in (0, 1):
            for d in (1, 2, 3):
                gather_copy(stage, r, d).wait_send()
                part_copy(stage, r, d).wait_send()

        @pl.when(cell < 31)
        def _():
            halo_copy(stage, 0).wait_send()

        @pl.when(cell > 0)
        def _():
            halo_copy(stage, 1).wait_send()


def on_device(populations, contact_mask, octant, courant, collision):
    dma = pltpu.SemaphoreType.DMA
    out = pl.pallas_call(
        kernel,
        out_shape=pltpu.VMEM((2 * B, B), F32),
        in_specs=[pl.BlockSpec(memory_space=pl.ANY)] * 5,
        out_specs=pl.BlockSpec(memory_space=pltpu.VMEM),
        scratch_shapes=[
            pltpu.VMEM((2 * B, B), F32),
            pltpu.VMEM((2, B), jnp.int32),
            pltpu.VMEM((1, B), jnp.int32),
            pltpu.VMEM((3, B), F32),
            pltpu.VMEM((5, B, B), F32),
            pltpu.VMEM((4, B, 4 * B), BF16),
            pltpu.VMEM((2, 2, 4 * B, B), BF16),
            pltpu.VMEM((2, 2, B, B), BF16),
            pltpu.VMEM((2, B, B), F32),
            pltpu.VMEM((2, 2, 3, B, B), BF16),
            pltpu.VMEM((2, 2, 3, B, B), BF16),
            pltpu.VMEM((2, 2, B, B), F32),
            dma((4,)),
            dma((4,)),
            dma((3, 4)),
            dma((3, 4)),
            dma((2, 2, 3)),
            dma((2, 2, 3)),
            dma((2, 2)),
            dma((2, 2)),
            dma((2, 2, 3)),
            dma((2, 2, 3)),
            pltpu.SemaphoreType.REGULAR,
        ],
        compiler_params=pltpu.CompilerParams(collective_id=0, has_side_effects=True),
        name="heun",
    )(
        populations.reshape(2 * B, B),
        contact_mask.reshape(2, B),
        octant.reshape(1, B),
        courant,
        collision,
    )
    return out.reshape(populations.shape)


def solution(mesh):
    placed = (
        P("mode", None, "cell", None),
        P(None, "cell", None),
        P("mode"),
        P(None, "mode"),
        P("mode", None),
    )
    return jax.shard_map(
        on_device,
        mesh=mesh,
        in_specs=placed,
        out_specs=P("mode", None, "cell", None),
        check_vma=False,
    )
```
